256 devices in a mesh: dp: 4 (over y), expert: 64 (over x, z, core).
Axes of the slice: x: 4, y: 4, z: 8, core: 2. Of those that a mesh axis runs over, the one named last changes fastest.
Arguments:
- tokens: bfloat16 [8192, 4096], P('expert', 'dp'), may hold values from -6 to 6
- cotangent: bfloat16 [8192, 4096], P('expert', 'dp'), may hold values from -1.5 to 1.5
- router_probs: bfloat16 [8192, 8], P('expert'), may hold values from 0.049804688 to 1
- expert_ids: int32 [8192, 8], P('expert'), may hold values from 0 to 63, all different within a row; in each aligned block of 128 rows (0 to 127, 128 to 255, ...) at most 17 rows name the same one
- w_gate: bfloat16 [64, 768, 4096], P('expert', None, 'dp'), may hold values from -0.09375 to 0.09375
- w_up: bfloat16 [64, 768, 4096], P('expert', None, 'dp'), may hold values from -0.09375 to 0.09375
- w_down: bfloat16 [64, 768, 4096], P('expert', None, 'dp'), may hold values from -0.21875 to 0.21875
Outputs:
- token_grads: bfloat16 [8192, 4096], P('expert', 'dp')
- prob_grads: float32 [8192, 8], P('expert')
- gate_grads: bfloat16 [64, 768, 4096], P('expert', None, 'dp')
- up_grads: bfloat16 [64, 768, 4096], P('expert', None, 'dp')
- down_grads: bfloat16 [64, 768, 4096], P('expert', None, 'dp')
The draws below stay inside these ranges and needn't reach their ends.
Inputs may be any that keep to these rules, and one draw needn't show every extreme that they name: `expert_ids`: each row names 8 different experts. Among the 128 tokens of one index of expert no expert is named more than 17 times, a bound that some block reaches.
All inputs are finite; a program needn't handle non-finite values.
Results may differ from the reference program's by a relative error of at most 0.02.
Values may be sent and summed in bfloat16 or wider, within the bound.
A program may use at most 128 MiB of HBM per device.

```python
import math
import jax
import jax.numpy as jnp
import numpy as np
from jax import lax

D = 4096
FF = 768
TOPK = 8
TOK_DEV = 128
EXPERTS = 64
TOKENS = 8192
SLOTS = 17
N_DP = 4
N_EXPERT = 64


def block_scale(rng, extent, shards, low, largest):
    loudness, own = 1.0, jax.random.fold_in(rng, 6)
    for dim, blocks in shards:
        heights = jnp.exp(jax.random.uniform(jax.random.fold_in(own, dim), (blocks,), jnp.float32, low / len(shards), largest / len(shards)))
        loudness = loudness * jnp.repeat(heights, extent[dim] // blocks).reshape([-1 if axis == dim else 1 for axis in range(len(extent))])
    return loudness


def assign_block(rng, own, number, rows, count, top, reach, slope):
    ranking = jax.random.permutation(rng, count)
    heavy_load, ordinary = shares(count, rows * top, reach, slope, True), shares(count, rows * top, reach, slope, False)
    places = jnp.arange(count)

    def named(lengths, rotation):
        used = int((lengths > 0).sum())
        fixed = max(1, used // 4)
        shifted = fixed + (places - fixed + rotation * (used - fixed)) % max(1, count - fixed)
        return jnp.zeros((count,), jnp.int32).at[ranking[jnp.where(places < fixed, places, shifted)]].set(jnp.asarray(lengths, jnp.int32))

    lengths = jnp.where(number % 4 == 0, named(heavy_load, number // 4), named(ordinary, number - number // 4 - 1))
    mixed = jax.random.permutation(jax.random.fold_in(own, 3), count)
    donor, taker = mixed[0:count // 2 * 2:2], mixed[1:count // 2 * 2:2]
    slack = jnp.minimum(lengths[donor] - 1, reach - lengths[taker]) // 2
    slack = jnp.where((donor == ranking[0]) | (taker == ranking[0]) | (lengths[taker] == 0), 0, jnp.maximum(slack, 0))
    shifted = jax.random.randint(jax.random.fold_in(own, 4), (count // 2,), 0, 1 << 20) % (slack + 1)
    lengths = lengths.at[donor].add(-shifted).at[taker].add(shifted)
    items = jnp.searchsorted(jnp.cumsum(lengths), jnp.arange(rows * top), side="right").astype(jnp.int32)
    grid = items.reshape(top, rows).T
    grid = grid[jax.random.permutation(jax.random.fold_in(own, 1), rows)]
    rotation = jax.random.randint(jax.random.fold_in(own, 2), (rows, 1), 0, top)
    return jnp.take_along_axis(grid, (jnp.arange(top)[None, :] + rotation) % top, axis=1)


def shares(count, total, limit, slope, full):
    portions = [(1 << 20) // math.isqrt(rank ** slope) + 1 for rank in range(1, count + 1)]
    largest = limit if full else min(limit, max(-(-total // count), total * portions[0] // sum(portions)))
    least = 1 if total - largest >= count - 1 else 0
    given, rest = [largest] + [least] * (count - 1), total - largest - least * (count - 1)
    while rest > 0:
        free = [i for i in range(1, count) if given[i] < largest] or [i for i in range(1, count) if given[i] < limit]
        pool, budget = sum([portions[i] for i in free]), rest
        for i in free:
            more = min(limit - given[i], max(1, budget * portions[i] // pool), rest)
            given[i] = given[i] + more
            rest = rest - more
    return np.array(given)


def scatter_about(key, shape, deviation, reach, cuts=(), held_as=jnp.bfloat16):
    factor_of = block_scale(key, shape, cuts, -0.22, 0.18) if cuts else 1.0
    drawn = jax.random.normal(key, shape, jnp.float32) * deviation * factor_of
    return jnp.minimum(jnp.maximum(drawn, -reach), reach).astype(held_as)


def setup_inputs(seed: int = 0) -> dict:
    key_of = jax.random.split(jax.random.key(seed), 8)
    tokens = scatter_about(key_of[0], (TOKENS, D), 1.0, 6.0, ((0, 64), (1, 4)))
    cotangent = scatter_about(key_of[1], (TOKENS, D), 0.25, 1.5, ((0, 64), (1, 4)))
    router_probs = jnp.clip(jnp.exp(math.log(1.0) - 2.9996462 * jax.random.uniform(key_of[2], (TOKENS, TOPK), jnp.float32) ** block_scale(key_of[2], (TOKENS, TOPK), ((0, 64),), -0.2, 0.2)), 0.049804688, 1.0).astype(jnp.bfloat16)
    expert_ids_keys = jax.random.split(jax.random.fold_in(key_of[3], 1), TOKENS // TOK_DEV)
    expert_ids_turns = jax.random.permutation(jax.random.fold_in(key_of[3], 3), TOKENS // TOK_DEV)
    expert_ids = jax.vmap(lambda own, number: assign_block(jax.random.fold_in(key_of[3], 2), own, number, TOK_DEV, EXPERTS, TOPK, SLOTS, 2))(expert_ids_keys, expert_ids_turns).reshape((TOKENS, TOPK))
    w_gate = scatter_about(key_of[4], (EXPERTS, FF, D), D ** -0.5, 0.09375, ((0, 64), (2, 4)))
    w_up = scatter_about(key_of[5], (EXPERTS, FF, D), D ** -0.5, 0.09375, ((0, 64), (2, 4)))
    w_down = scatter_about(key_of[6], (EXPERTS, FF, D), FF ** -0.5, 0.21875, ((0, 64), (2, 4)))
    return dict(tokens=tokens, cotangent=cotangent, router_probs=router_probs, expert_ids=expert_ids, w_gate=w_gate, w_up=w_up, w_down=w_down)


def contract_last(left_matrix, right_matrix):
    return lax.dot_general(left_matrix, right_matrix, (((1,), (1,)), ((), ())), preferred_element_type=jnp.float32)


def contract_first(left_matrix, right_matrix):
    return lax.dot_general(left_matrix, right_matrix, (((0,), (0,)), ((), ())), preferred_element_type=jnp.float32)


def rounded(values):
    return lax.optimization_barrier(values.astype(jnp.bfloat16)).astype(jnp.float32)


def block_sum(rows, weight):
    width = D // N_DP
    total = jnp.zeros((rows.shape[0], weight.shape[0]), jnp.float32)
    for block_index in range(N_DP):
        low = block_index * width
        total = total + rounded(contract_last(rows[:, low:low + width], weight[:, low:low + width]))
    return total


def reference(tokens, cotangent, router_probs, expert_ids, w_gate, w_up, w_down):
    total_rows = TOKENS * TOPK
    flat_ids = expert_ids.reshape(-1)
    flat_probs = router_probs.reshape(-1)
    capacity = N_EXPERT * SLOTS
    zero_value = jnp.zeros((), tokens.dtype)

    def per_expert(state_pair, expert):
        token_acc, prob_acc = state_pair
        row_index = jnp.nonzero(flat_ids == expert, size=capacity, fill_value=total_rows)[0].astype(jnp.int32)
        valid = row_index < total_rows
        safe_rows = jnp.minimum(row_index, total_rows - 1)
        owners = safe_rows // TOPK
        inputs = jnp.where(valid[:, None], tokens[owners], zero_value)
        grads_in = jnp.where(valid[:, None], cotangent[owners], zero_value)
        weights = jnp.where(valid, flat_probs[safe_rows], jnp.zeros((), router_probs.dtype)).astype(jnp.float32)
        weight_gate = w_gate[expert]
        weight_up = w_up[expert]
        weight_down = w_down[expert]
        gate_value = block_sum(inputs, weight_gate)
        up_value = block_sum(inputs, weight_up)
        back_value = block_sum(grads_in, weight_down)
        sigmoid_gate = jax.nn.sigmoid(gate_value)
        silu_gate = gate_value * sigmoid_gate
        hidden = (silu_gate * up_value).astype(jnp.bfloat16)
        prob_value = rounded(jnp.sum(hidden.astype(jnp.float32) * back_value, axis=1))
        row_scale = weights[:, None]
        grad_back = row_scale * back_value
        grad_gate = (grad_back * up_value * sigmoid_gate * (1.0 + gate_value * (1.0 - sigmoid_gate))).astype(jnp.bfloat16)
        grad_up = (grad_back * silu_gate).astype(jnp.bfloat16)
        scaled = (row_scale * grads_in.astype(jnp.float32)).astype(jnp.bfloat16)
        row_term = jnp.dot(grad_gate, weight_gate, preferred_element_type=jnp.float32)
        row_term = rounded(row_term + jnp.dot(grad_up, weight_up, preferred_element_type=jnp.float32))
        token_acc = token_acc.at[owners].add(jnp.where(valid[:, None], row_term, 0.0))
        prob_acc = prob_acc.at[safe_rows].add(jnp.where(valid, prob_value, 0.0))
        gate_grad = contract_first(grad_gate, inputs).astype(jnp.bfloat16)
        up_grad = contract_first(grad_up, inputs).astype(jnp.bfloat16)
        down_grad = contract_first(hidden, scaled).astype(jnp.bfloat16)
        return (token_acc, prob_acc), (gate_grad, up_grad, down_grad)

    start_pair = (jnp.zeros((TOKENS, D), jnp.float32), jnp.zeros((total_rows,), jnp.float32))
    final_pair, weight_grads = lax.scan(per_expert, start_pair, jnp.arange(EXPERTS, dtype=jnp.int32))
    token_grads = final_pair[0].astype(jnp.bfloat16)
    prob_grads = final_pair[1].reshape(TOKENS, TOPK)
    return token_grads, prob_grads, weight_grads[0], weight_grads[1], weight_grads[2]
```

```python
import functools
import types

import jax
import jax.numpy as jnp
from jax import lax
from jax.experimental import pallas as pl
from jax.experimental.pallas import tpu as pltpu
from jax.sharding import PartitionSpec as P

MESH = pl.DeviceIdType.MESH
LANES = 128
MAIN = 16
SPARE = 8
F32 = jnp.float32
BF16 = jnp.bfloat16


def dot(left, right, left_dim, right_dim):
    return lax.dot_general(
        left, right, (((left_dim,), (right_dim,)), ((), ())), preferred_element_type=F32
    )


def make_layout(n_x, n_z, n_core, rounds):
    order = [k for ks, _ in rounds for k in ks]
    return types.SimpleNamespace(
        n_x=n_x,
        n_z=n_z,
        n_core=n_core,
        peers=n_x * n_core,
        rounds=rounds,
        place={k: i for i, k in enumerate(order)},
        order=order,
    )


def kernel(lay, steps, tok, cot, aux, wg, wu, wd, tg_out, pg_out, gg_out, ug_out, dg_out, *scratch):
    (
        tok_all, cot_all, aux_all, hot, hot_spare, hot_spare_p, sent, sent_spare, rows, rows_spare,
        weights, part, part_spare, first, first_spare, second, second_spare, acts, acts_spare,
        term, term_spare, back, back_spare, z_sent, z_right, z_left, pg_sent, pg_got, grads,
        w_sem, own_sem, out_sem, aux_ss, aux_rs, ag_ss, ag_rs, d_ss, d_rs, y_ss, y_rs, yo_ss, yo_rs,
        t_ss, t_rs, z_ss, z_rs, pg_ss, pg_rs,
    ) = scratch
    n_z, peers, n_core = lay.n_z, lay.peers, lay.n_core
    n_tok, feats = tok.shape
    units = wg.shape[0]
    row_w = 2 * feats + LANES
    act_w = 3 * units + LANES
    term_w = feats + LANES
    half = 3 * units // 2
    act_half = ((act_w // LANES + 1) // 2) * LANES
    per = peers // 4
    far = n_z // 2
    y = lax.axis_index("dp")
    e = lax.axis_index("expert")
    x, z, core = e // (n_z * n_core), (e // n_core) % n_z, e % n_core
    me = x * n_core + core

    def place_of(peer, plane):
        return ((peer // n_core) * n_z + plane) * n_core + peer % n_core

    z_next = (y, place_of(me, (z + 1) % n_z))
    z_prev = (y, place_of(me, (z + n_z - 1) % n_z))
    y_next = ((y + 1) % 4, e)
    y_prev = ((y + 3) % 4, e)
    right_y, left_y, across_y = (y + 1) % 4, (y + 3) % 4, (y + 2) % 4

    def remote(src, dst, send_sem, recv_sem, device):
        return pltpu.make_async_remote_copy(
            src_ref=src, dst_ref=dst, send_sem=send_sem, recv_sem=recv_sem,
            device_id=device, device_id_type=MESH,
        )

    pending = []

    def go(copy):
        copy.start()
        pending.append(copy)
        return copy

    loads = [
        pltpu.make_async_copy(w, weights.at[pl.ds(i * units, units)], w_sem.at[i])
        for i, w in enumerate((wg, wu, wd))
    ]
    own = [
        pltpu.make_async_copy(tok, tok_all.at[0], own_sem.at[0]),
        pltpu.make_async_copy(cot, cot_all.at[0], own_sem.at[1]),
        pltpu.make_async_copy(aux, aux_all.at[0], own_sem.at[2]),
    ]
    for copy in own + loads:
        copy.start()

    barrier = pltpu.get_barrier_semaphore()
    for device in (y_next, y_prev):
        pl.semaphore_signal(barrier, inc=1, device_id=device, device_id_type=MESH)
    for k in range(1, n_z):
        pl.semaphore_signal(
            barrier, inc=1, device_id=(y, place_of(me, (z + k) % n_z)), device_id_type=MESH
        )
    for k in range(1, peers):
        pl.semaphore_signal(
            barrier, inc=1, device_id=(y, place_of((me + k) % peers, z)), device_id_type=MESH
        )
    pl.semaphore_wait(barrier, 2 + n_z - 1 + peers - 1)

    def z_span(hop, way):
        if hop < far:
            return pl.ds(0, n_tok)
        return pl.ds(0 if way == 0 else n_tok // 2, n_tok // 2)

    def z_hop(hop, way):
        sign = -1 if way == 0 else 1
        src_slot, dst_slot = (sign * (hop - 1)) % n_z, (sign * hop) % n_z
        span = z_span(hop, way)
        out = []
        for i, (mine, held) in enumerate(((tok, tok_all), (cot, cot_all))):
            src = mine.at[span] if hop == 1 else held.at[src_slot, span]
            out.append(
                remote(
                    src, held.at[dst_slot, span], ag_ss.at[way, hop - 1, i],
                    ag_rs.at[way, hop - 1, i], z_next if way == 0 else z_prev,
                )
            )
        return out

    arrived = {}

    def z_send(hop):
        for way in (0, 1):
            arrived[hop, way] = [go(copy) for copy in z_hop(hop, way)]

    def z_wait(hop, ways=(0, 1)):
        for way in ways:
            for copy in arrived[hop, way]:
                copy.wait_recv()

    aux_copies = {}

    def aux_send():
        for k in range(1, n_z):
            aux_copies[k] = go(
                remote(
                    aux, aux_all.at[k], aux_ss.at[k], aux_rs.at[k],
                    (y, place_of(me, (z + n_z - k) % n_z)),
                )
            )

    names = [place_of(j, z) for j in range(peers)]

    def read_table(slot):
        table = aux_all[slot]
        ids = table[0:8].astype(jnp.int32)
        return ids, table[8:16]

    def pick(pos, slot):
        ids, probs = read_table(slot)
        hits = jnp.concatenate(
            [jnp.sum(jnp.where(ids == n, 1.0, 0.0), axis=0, keepdims=True) for n in names], axis=0
        )
        given = [jnp.sum(jnp.where(ids == n, probs, 0.0), axis=0, keepdims=True) for n in names]
        before = (
            lax.broadcasted_iota(jnp.int32, (n_tok, n_tok), 0)
            < lax.broadcasted_iota(jnp.int32, (n_tok, n_tok), 1)
        )
        if peers % 8:
            hits_full = jnp.concatenate([hits, jnp.zeros((8 - peers, n_tok), F32)], axis=0)
        else:
            hits_full = hits
        rank = dot(hits_full.astype(BF16), jnp.where(before, 1.0, 0.0).astype(BF16), 1, 0)
        rank = jnp.where(hits > 0.5, rank[0:peers], -1.0)
        s_main = lax.broadcasted_iota(jnp.int32, (MAIN, n_tok), 0).astype(F32)
        s_spare = lax.broadcasted_iota(jnp.int32, (SPARE, n_tok), 0)
        main, main_p, spare, spare_p = [], [], [], []
        for j in range(peers):
            r = rank[j : j + 1]
            one = jnp.where(jnp.broadcast_to(r, (MAIN, n_tok)) == s_main, 1.0, 0.0)
            main.append(one)
            main_p.append(one * jnp.broadcast_to(given[j], (MAIN, n_tok)))
            over = jnp.where(r > MAIN - 0.5, 1.0, 0.0)
            sp = jnp.where(s_spare == slot, jnp.broadcast_to(over, (SPARE, n_tok)), 0.0)
            spare.append(sp)
            spare_p.append(sp * jnp.broadcast_to(given[j], (SPARE, n_tok)))
        one = jnp.concatenate(main, axis=0).astype(BF16)
        hot[pos] = one
        cols = pl.ds(slot * n_tok, n_tok)
        hot_spare[:, cols] = jnp.concatenate(spare, axis=0).astype(BF16)
        hot_spare_p[:, cols] = jnp.concatenate(spare_p, axis=0).astype(BF16)
        ones = jnp.ones((n_tok, LANES), BF16)
        shape = (peers, MAIN, -1)
        probs_rows = dot(jnp.concatenate(main_p, axis=0).astype(BF16), ones, 1, 0)
        sent[pos, :, :, 2 * feats :] = probs_rows.astype(BF16).reshape(peers, MAIN, LANES)
        sent[pos, :, :, 0:feats] = dot(one, tok_all[slot], 1, 0).astype(BF16).reshape(peers, MAIN, feats)
        sent[pos, :, :, feats : 2 * feats] = (
            dot(one, cot_all[slot], 1, 0).astype(BF16).reshape(peers, MAIN, feats)
        )

    def exchange(src, dst, send_sems, recv_sems, row):
        def copy_to(i):
            j = (me + i) % peers
            return remote(
                src.at[j], dst.at[me], send_sems.at[row, i], recv_sems.at[row, me],
                (y, place_of(j, z)),
            )

        def copy_from(i):
            j = (me + i) % peers
            return remote(
                src.at[j], dst.at[j], send_sems.at[row, i], recv_sems.at[row, j],
                (y, place_of(j, z)),
            )

        def start():
            @pl.loop(1, peers)
            def _(i):
                copy_to(i).start()

            dst[pl.ds(me, 1)] = src[pl.ds(me, 1)]

        def wait():
            @pl.loop(1, peers)
            def _(i):
                copy_from(i).wait_recv()

        def finish():
            @pl.loop(1, peers)
            def _(i):
                copy_to(i).wait_send()

        return types.SimpleNamespace(start=start, wait=wait, finish=finish)

    n_pos = len(lay.order)
    dispatch = {
        k: exchange(sent.at[p], rows.at[p], d_ss, d_rs, p) for k, p in lay.place.items()
    }
    dispatch_spare = exchange(sent_spare, rows_spare, d_ss, d_rs, n_pos)
    ret = {k: exchange(term.at[p], back.at[p], t_ss, t_rs, p) for k, p in lay.place.items()}
    ret_spare = exchange(term_spare, back_spare, t_ss, t_rs, n_pos)

    def gather(k):
        if k:
            aux_copies[k % n_z].wait_recv()
        pick(lay.place[k], k % n_z)
        dispatch[k].start()

    def gather_spare():
        ones = jnp.ones((n_z * n_tok, LANES), BF16)
        shape = (peers, SPARE)
        sent_spare[:, :, 2 * feats :] = (
            dot(hot_spare_p[...], ones, 1, 0).astype(BF16).reshape(shape + (LANES,))
        )
        for i, held in enumerate((tok_all, cot_all)):
            block = held[...].reshape(n_z * n_tok, feats)
            sent_spare[:, :, i * feats : (i + 1) * feats] = (
                dot(hot_spare[...], block, 1, 0).astype(BF16).reshape(shape + (feats,))
            )
        dispatch_spare.start()

    tile = min(256, units)

    def segment(r):
        ks, spare = lay.rounds[r]
        first_pos = lay.place[ks[0]]
        return pl.ds(first_pos, len(ks)), len(ks), spare

    y_copies = {}

    def y_send(kind, r, way, src, dst, src_spare, dst_spare, spare):
        device = y_next if way == 0 else y_prev
        made = [go(remote(src, dst, y_ss.at[kind, r, way], y_rs.at[kind, r, way], device))]
        if spare:
            made.append(
                go(remote(src_spare, dst_spare, yo_ss.at[kind, way], yo_rs.at[kind, way], device))
            )
        y_copies[kind, r, way] = made

    def y_wait(kind, r, way):
        for copy in y_copies[kind, r, way]:
            copy.wait_recv()

    def shard(index):
        return pl.ds(index * per, per)

    def project(r):
        span, n, spare = segment(r)
        for k in lay.rounds[r][0]:
            dispatch[k].wait()
        if spare:
            dispatch_spare.wait()
        if r == 0:
            for copy in loads:
                copy.wait()
        for base, count, col in ((0, 2 * units // tile, 0), (2 * units, units // tile, feats)):
            @pl.loop(0, count)
            def _(i):
                at = pl.multiple_of(base + i * tile, tile)
                block = weights[pl.ds(at, tile)]
                left = rows[span, :, :, col : col + feats].reshape(n * peers * MAIN, feats)
                out = dot(left, block, 1, 1).astype(BF16)
                part[span, :, :, pl.ds(at, tile)] = out.reshape(n, peers, MAIN, tile)
                if spare:
                    left = rows_spare[:, :, col : col + feats].reshape(peers * SPARE, feats)
                    out = dot(left, block, 1, 1).astype(BF16)
                    part_spare[:, :, pl.ds(at, tile)] = out.reshape(4, peers * SPARE // 4, tile)
        for way, cols in ((0, pl.ds(0, half)), (1, pl.ds(half, half))):
            y_send(
                0, r, way, part.at[span, shard(across_y), :, cols], first.at[way, span],
                part_spare.at[across_y, :, cols], first_spare.at[way], spare,
            )

    def fold(r):
        span, n, spare = segment(r)
        for way, cols, owner in ((0, pl.ds(0, half), right_y), (1, pl.ds(half, half), left_y)):
            y_wait(0, r, way)
            part[span, shard(owner), :, cols] = (
                part[span, shard(owner), :, cols].astype(F32) + first[way, span].astype(F32)
            ).astype(BF16)
            if spare:
                part_spare[pl.ds(owner, 1), :, cols] = (
                    part_spare[pl.ds(owner, 1), :, cols].astype(F32)
                    + first_spare[pl.ds(way, 1)].astype(F32)
                ).astype(BF16)
            y_send(
                1, r, way, part.at[span, shard(owner)], second.at[way, span],
                part_spare.at[owner], second_spare.at[way], spare,
            )

    def act_math(values, probs, units_w):
        gate, up, bck = values
        s = jax.nn.sigmoid(gate)
        silu = gate * s
        hidden = (silu * up).astype(BF16)
        pv = jnp.sum(hidden.astype(F32) * bck, axis=1, keepdims=True)
        p = jnp.concatenate([probs.astype(F32)] * (units_w // LANES), axis=1)
        gb = p * bck
        d_gate = (gb * up * s * (1.0 + gate * (1.0 - s))).astype(BF16)
        d_up = (gb * silu).astype(BF16)
        return hidden, d_gate, d_up, jnp.broadcast_to(pv, (pv.shape[0], LANES)).astype(BF16)

    def activate(r):
        span, n, spare = segment(r)
        y_wait(1, r, 0)
        y_wait(1, r, 1)
        count = n * per * MAIN

        def value(i):
            cols = pl.ds(i * units, units)
            return (
                part[span, shard(y), :, cols].astype(F32)
                + second[0, span, :, :, cols].astype(F32)
                + second[1, span, :, :, cols].astype(F32)
            ).reshape(count, units)

        probs = rows[span, shard(y), :, 2 * feats :].reshape(count, LANES)
        hidden, d_gate, d_up, pv = act_math([value(i) for i in range(3)], probs, units)
        for i, v in enumerate((hidden, d_gate, d_up)):
            acts[span, shard(y), :, i * units : (i + 1) * units] = v.reshape(n, per, MAIN, units)
        acts[span, shard(y), :, 3 * units :] = pv.reshape(n, per, MAIN, LANES)
        if spare:
            count = per * SPARE

            def value_spare(i):
                cols = pl.ds(i * units, units)
                return (
                    part_spare[pl.ds(y, 1), :, cols].astype(F32)
                    + second_spare[pl.ds(0, 1), :, cols].astype(F32)
                    + second_spare[pl.ds(1, 1), :, cols].astype(F32)
                ).reshape(count, units)

            probs = rows_spare[shard(y), :, 2 * feats :].reshape(count, LANES)
            hidden, d_gate, d_up, pv = act_math([value_spare(i) for i in range(3)], probs, units)
            for i, v in enumerate((hidden, d_gate, d_up)):
                acts_spare[pl.ds(y, 1), :, i * units : (i + 1) * units] = v.reshape(1, count, units)
            acts_spare[pl.ds(y, 1), :, 3 * units :] = pv.reshape(1, count, LANES)
        for way in (0, 1):
            y_send(
                2, r, way, acts.at[span, shard(y)], acts.at[span, shard(y)],
                acts_spare.at[y], acts_spare.at[y], spare,
            )

    def relay(r):
        span, n, spare = segment(r)
        for way, cols, owner in (
            (0, pl.ds(0, act_half), left_y), (1, pl.ds(act_half, act_w - act_half), right_y)
        ):
            y_wait(2, r, way)
            y_send(
                3, r, way, acts.at[span, shard(owner), :, cols], acts.at[span, shard(owner), :, cols],
                acts_spare.at[owner, :, cols], acts_spare.at[owner, :, cols], spare,
            )

    f_tile = min(256, feats)

    def send_back(r):
        span, n, spare = segment(r)
        y_wait(3, r, 0)
        y_wait(3, r, 1)

        @pl.loop(0, feats // f_tile)
        def _(i):
            at = pl.multiple_of(i * f_tile, f_tile)
            block = weights[0 : 2 * units, pl.ds(at, f_tile)]
            left = acts[span, :, :, units : 3 * units].reshape(n * peers * MAIN, 2 * units)
            term[span, :, :, pl.ds(at, f_tile)] = (
                dot(left, block, 1, 0).astype(BF16).reshape(n, peers, MAIN, f_tile)
            )
            if spare:
                left = acts_spare[:, :, units : 3 * units].reshape(peers * SPARE, 2 * units)
                term_spare[:, :, pl.ds(at, f_tile)] = (
                    dot(left, block, 1, 0).astype(BF16).reshape(peers, SPARE, f_tile)
                )

        term[span, :, :, feats:] = acts[span, :, :, 3 * units :]
        for k in lay.rounds[r][0]:
            ret[k].start()
        if spare:
            term_spare[:, :, feats:] = acts_spare[:, :, 3 * units :].reshape(peers, SPARE, LANES)
            ret_spare.start()

    z_copies = {}
    pg_copies = {}

    def wait_spare():
        ret_spare.wait()

    def combine(k):
        pos, slot = lay.place[k], k % n_z
        ret[k].wait()
        got = back[pos].reshape(peers * MAIN, term_w)
        got_spare = back_spare[...].reshape(peers * SPARE, term_w)
        one = hot[pos]
        spare = hot_spare[:, pl.ds(slot * n_tok, n_tok)]
        total = dot(one, got[:, 0:feats], 0, 0) + dot(spare, got_spare[:, 0:feats], 0, 0)
        ids, _ = read_table(slot)
        weighted = one.astype(F32) * got[:, feats:].astype(F32)
        weighted_spare = spare.astype(F32) * got_spare[:, feats:].astype(F32)
        grad = jnp.zeros((8, n_tok), F32)
        for j in range(peers):
            v = jnp.sum(weighted[j * MAIN : (j + 1) * MAIN], axis=0, keepdims=True)
            v = v + jnp.sum(weighted_spare[j * SPARE : (j + 1) * SPARE], axis=0, keepdims=True)
            grad = grad + jnp.where(ids == names[j], jnp.broadcast_to(v, (8, n_tok)), 0.0)
        if k == 0:
            pg_got[0] = grad
        else:
            pg_sent[slot] = grad
            pg_copies[slot] = go(
                remote(
                    pg_sent.at[slot], pg_got.at[n_z - slot], pg_ss.at[slot], pg_rs.at[n_z - slot],
                    (y, place_of(me, (z + slot) % n_z)),
                )
            )
        k_signed = k if k <= far else k - n_z
        if k_signed == far:
            z_sent[slot] = total.astype(BF16)
            lo, hi = pl.ds(0, n_tok // 2), pl.ds(n_tok // 2, n_tok // 2)
            z_copies[0, far] = go(
                remote(z_sent.at[slot, lo], z_right.at[far - 1, lo], z_ss.at[0, far],
                       z_rs.at[0, far - 1], z_next)
            )
            z_copies[1, far] = go(
                remote(z_sent.at[slot, hi], z_left.at[far - 1, hi], z_ss.at[1, far],
                       z_rs.at[1, far - 1], z_prev)
            )
            return
        h = n_tok // 2
        if k_signed != 0:
            way = 0 if k_signed > 0 else 1
            dist = abs(k_signed)
            z_copies[way, dist + 1].wait_recv()
            held = z_right if way == 0 else z_left
            if dist == far - 1:
                if way == 0:
                    z_sent[slot, 0:h] = (total[0:h] + held[dist, 0:h].astype(F32)).astype(BF16)
                    z_sent[slot, h:] = total[h:].astype(BF16)
                else:
                    z_sent[slot, h:] = (total[h:] + held[dist, h:].astype(F32)).astype(BF16)
                    z_sent[slot, 0:h] = total[0:h].astype(BF16)
            else:
                z_sent[slot] = (total + held[dist].astype(F32)).astype(BF16)
            z_copies[way, dist] = go(
                remote(z_sent.at[slot], held.at[dist - 1], z_ss.at[way, dist],
                       z_rs.at[way, dist - 1], z_next if way == 0 else z_prev)
            )
            return
        z_copies[0, 1].wait_recv()
        z_copies[1, 1].wait_recv()
        tg_out[...] = (total + z_right[0].astype(F32) + z_left[0].astype(F32)).astype(BF16)

    def finish_probs():
        for slot in pg_copies:
            pg_copies[slot].wait_recv()
        total = pg_got[0]
        for slot in range(1, n_z):
            total = total + pg_got[slot]
        pg_out[...] = total

    outs = [
        pltpu.make_async_copy(grads.at[pl.ds(i * units, units)], o, out_sem.at[i])
        for i, o in enumerate((gg_out, ug_out, dg_out))
    ]

    all_rows = n_pos * peers * MAIN

    def grads_in():
        left_full = rows[:, :, :, 0:feats].reshape(all_rows, feats)
        left_spare = rows_spare[:, :, 0:feats].reshape(peers * SPARE, feats)

        @pl.loop(0, 2 * units // tile)
        def _(i):
            at = pl.multiple_of(units + i * tile, tile)
            a = acts[:, :, :, pl.ds(at, tile)].reshape(all_rows, tile)
            b = acts_spare[:, :, pl.ds(at, tile)].reshape(peers * SPARE, tile)
            full = rows[:, :, :, 0:feats].reshape(all_rows, feats)
            spare = rows_spare[:, :, 0:feats].reshape(peers * SPARE, feats)
            grads[pl.ds(pl.multiple_of(i * tile, tile), tile)] = (
                dot(a, full, 0, 0) + dot(b, spare, 0, 0)
            ).astype(BF16)

        outs[0].start()
        outs[1].start()

    def scale():
        @pl.loop(0, n_pos)
        def _(i):
            p = rows[pl.ds(i, 1), :, :, 2 * feats :].astype(F32)
            p = jnp.concatenate([p] * (feats // LANES), axis=3)
            c = rows[pl.ds(i, 1), :, :, feats : 2 * feats].astype(F32)
            rows[pl.ds(i, 1), :, :, feats : 2 * feats] = (p * c).astype(BF16)

        p = jnp.concatenate([rows_spare[:, :, 2 * feats :].astype(F32)] * (feats // LANES), axis=2)
        c = rows_spare[:, :, feats : 2 * feats].astype(F32)
        rows_spare[:, :, feats : 2 * feats] = (p * c).astype(BF16)

    def grads_down():
        @pl.loop(0, units // tile)
        def _(i):
            at = pl.multiple_of(i * tile, tile)
            a = acts[:, :, :, pl.ds(at, tile)].reshape(all_rows, tile)
            b = acts_spare[:, :, pl.ds(at, tile)].reshape(peers * SPARE, tile)
            full = rows[:, :, :, feats : 2 * feats].reshape(all_rows, feats)
            spare = rows_spare[:, :, feats : 2 * feats].reshape(peers * SPARE, feats)
            grads[pl.ds(pl.multiple_of(2 * units + i * tile, tile), tile)] = (
                dot(a, full, 0, 0) + dot(b, spare, 0, 0)
            ).astype(BF16)

        outs[2].start()

    def own_wait():
        for copy in own:
            copy.wait()

    table = dict(
        aux_send=aux_send, z_send=z_send, z_wait=z_wait, own_wait=own_wait, gather=gather,
        gather_spare=gather_spare, project=project, fold=fold, activate=activate, relay=relay,
        send_back=send_back, wait_spare=wait_spare, combine=combine, finish_probs=finish_probs,
        grads_in=grads_in, scale=scale, grads_down=grads_down,
    )
    for name, *args in steps:
        table[name](*args)
    for copy in outs:
        copy.wait()
    for copy in pending:
        copy.wait_send()
    for group in (dispatch, ret):
        for item in group.values():
            item.finish()
    dispatch_spare.finish()
    ret_spare.finish()


def plan(n_z):
    if n_z == 4:
        rounds = [([0], False), ([2, 1], True), ([-1], False)]
        steps = [
            ("aux_send",), ("z_send", 1), ("own_wait",), ("gather", 0),
            ("z_wait", 1), ("z_send", 2), ("gather", 1), ("gather", -1), ("project", 0), ("fold", 0),
            ("activate", 0), ("z_wait", 2), ("gather", 2), ("gather_spare",), ("relay", 0),
            ("project", 1), ("fold", 1), ("send_back", 0), ("activate", 1), ("project", 2),
            ("relay", 1), ("fold", 2), ("send_back", 1), ("activate", 2), ("wait_spare",),
            ("combine", 2), ("combine", 1), ("relay", 2), ("scale",),
            ("send_back", 2), ("grads_in",), ("combine", -1), ("combine", 0), ("grads_down",),
            ("finish_probs",),
        ]
        return rounds, steps
    rounds = [([0], False), ([1], False), ([2, -2], False), ([3, 4], True), ([-3], False), ([-1], False)]
    steps = [
        ("aux_send",), ("z_send", 1), ("own_wait",), ("gather", 0),
        ("project", 0), ("fold", 0),
        ("z_wait", 1), ("z_send", 2), ("gather", 1), ("gather", -1),
        ("activate", 0), ("relay", 0),
        ("z_wait", 2), ("z_send", 3), ("gather", 2), ("gather", -2),
        ("project", 1), ("send_back", 0), ("fold", 1), ("activate", 1),
        ("z_wait", 3), ("z_send", 4), ("gather", 3), ("gather", -3), ("relay", 1),
        ("project", 2), ("send_back", 1), ("fold", 2),
        ("z_wait", 4), ("gather", 4), ("gather_spare",),
        ("activate", 2), ("project", 3), ("relay", 2), ("fold", 3), ("send_back", 2),
        ("activate", 3), ("project", 4), ("fold", 4), ("relay", 3), ("activate", 4), ("project", 5),
        ("send_back", 3), ("fold", 5), ("relay", 4), ("scale",), ("activate", 5),
        ("wait_spare",), ("combine", 4), ("send_back", 4), ("combine", 3),
        ("relay", 5), ("combine", -3), ("combine", 2), ("combine", -2), ("send_back", 5),
        ("combine", 1), ("grads_in",), ("combine", -1), ("grads_down",), ("combine", 0),
        ("finish_probs",),
    ]
    return rounds, steps


def build(n_x, n_z, n_core):
    rounds, steps = plan(n_z)
    lay = make_layout(n_x, n_z, n_core, rounds)

    def local(tokens, cotangent, router_probs, expert_ids, w_gate, w_up, w_down):
        n_tok, feats = tokens.shape
        units = w_gate.shape[1]
        peers, n_pos, per = lay.peers, n_z, lay.peers // 4
        row_w, act_w, term_w = 2 * feats + LANES, 3 * units + LANES, feats + LANES
        extra = 8 - expert_ids.shape[1]
        aux = jnp.concatenate(
            [
                jnp.pad(expert_ids.T.astype(F32), ((0, extra), (0, 0)), constant_values=-1.0),
                jnp.pad(router_probs.T.astype(F32), ((0, extra), (0, 0))),
            ],
            axis=0,
        )
        half = 3 * units // 2
        spare_rows = peers * SPARE // 4
        dma = pltpu.SemaphoreType.DMA
        n_r = len(rounds)
        vm = pltpu.VMEM
        scratch = [
            vm((n_z, n_tok, feats), BF16), vm((n_z, n_tok, feats), BF16), vm((n_z, 16, n_tok), F32),
            vm((n_pos, peers * MAIN, n_tok), BF16), vm((peers * SPARE, n_z * n_tok), BF16),
            vm((peers * SPARE, n_z * n_tok), BF16),
            vm((n_pos, peers, MAIN, row_w), BF16), vm((peers, SPARE, row_w), BF16),
            vm((n_pos, peers, MAIN, row_w), BF16), vm((peers, SPARE, row_w), BF16),
            vm((3 * units, feats), BF16),
            vm((n_pos, peers, MAIN, 3 * units), BF16), vm((4, spare_rows, 3 * units), BF16),
            vm((2, n_pos, per, MAIN, half), BF16), vm((2, spare_rows, half), BF16),
            vm((2, n_pos, per, MAIN, 3 * units), BF16), vm((2, spare_rows, 3 * units), BF16),
            vm((n_pos, peers, MAIN, act_w), BF16), vm((4, spare_rows, act_w), BF16),
            vm((n_pos, peers, MAIN, term_w), BF16), vm((peers, SPARE, term_w), BF16),
            vm((n_pos, peers, MAIN, term_w), BF16), vm((peers, SPARE, term_w), BF16),
            vm((n_z, n_tok, feats), BF16), vm((n_z // 2, n_tok, feats), BF16),
            vm((n_z // 2, n_tok, feats), BF16),
            vm((n_z, 8, n_tok), F32), vm((n_z, 8, n_tok), F32), vm((3 * units, feats), BF16),
            dma((3,)), dma((3,)), dma((3,)), dma((n_z,)), dma((n_z,)),
            dma((2, n_z // 2, 2)), dma((2, n_z // 2, 2)),
            dma((n_pos + 1, peers)), dma((n_pos + 1, peers)),
            dma((4, n_r, 2)), dma((4, n_r, 2)), dma((4, 2)), dma((4, 2)),
            dma((n_pos + 1, peers)), dma((n_pos + 1, peers)),
            dma((2, n_z // 2 + 1)), dma((2, n_z // 2 + 1)), dma((n_z,)), dma((n_z,)),
        ]
        sds = jax.ShapeDtypeStruct
        anywhere = pl.BlockSpec(memory_space=pl.ANY)
        inside = pl.BlockSpec(memory_space=pltpu.VMEM)
        tg, pg, gg, ug, dg = pl.pallas_call(
            functools.partial(kernel, lay, steps),
            out_shape=(
                sds((n_tok, feats), BF16), sds((8, n_tok), F32), sds((units, feats), BF16),
                sds((units, feats), BF16), sds((units, feats), BF16),
            ),
            in_specs=[anywhere] * 6,
            out_specs=(inside, inside, anywhere, anywhere, anywhere),
            scratch_shapes=scratch,
            compiler_params=pltpu.CompilerParams(
                collective_id=0, has_side_effects=True, vmem_limit_bytes=63 * 1024 * 1024
            ),
        )(tokens, cotangent, aux, w_gate[0], w_up[0], w_down[0])
        return tg, pg[: expert_ids.shape[1]].T, gg[None], ug[None], dg[None]

    return local


def solution(mesh, shape=(4, 8, 2)):
    return jax.shard_map(
        build(*shape),
        mesh=mesh,
        in_specs=(
            P("expert", "dp"), P("expert", "dp"), P("expert", None), P("expert", None),
            P("expert", None, "dp"), P("expert", None, "dp"), P("expert", None, "dp"),
        ),
        out_specs=(
            P("expert", "dp"), P("expert", None),
            P("expert", None, "dp"), P("expert", None, "dp"), P("expert", None, "dp"),
        ),
        check_vma=False,
    )
```

```python
import functools
import types

import jax
import jax.numpy as jnp
from jax import lax
from jax.experimental import pallas as pl
from jax.experimental.pallas import tpu as pltpu
from jax.sharding import PartitionSpec as P

MESH = pl.DeviceIdType.MESH
LANES = 128
MAIN = 16
SPARE = 8
F32 = jnp.float32
BF16 = jnp.bfloat16


def dot(left, right, left_dim, right_dim):
    return lax.dot_general(
        left, right, (((left_dim,), (right_dim,)), ((), ())), preferred_element_type=F32
    )


def make_layout(n_x, n_z, n_core, rounds):
    order = [k for ks, _ in rounds for k in ks]
    return types.SimpleNamespace(
        n_x=n_x,
        n_z=n_z,
        n_core=n_core,
        peers=n_x * n_core,
        rounds=rounds,
        place={k: i for i, k in enumerate(order)},
        order=order,
    )


def kernel(lay, steps, tok, cot, aux, wg, wu, wd, tg_out, pg_out, gg_out, ug_out, dg_out, *scratch):
    (
        tok_all, cot_all, aux_all, hot, hot_spare, hot_spare_p, sent, sent_spare, rows, rows_spare,
        weights, part, part_spare, first, first_spare, second, second_spare, acts, acts_spare,
        term, term_spare, back, back_spare, z_sent, z_right, z_left, pg_sent, pg_got, grads,
        w_sem, own_sem, out_sem, aux_ss, aux_rs, ag_ss, ag_rs, d_ss, d_rs, y_ss, y_rs, yo_ss, yo_rs,
        t_ss, t_rs, z_ss, z_rs, pg_ss, pg_rs,
    ) = scratch
    n_z, peers, n_core = lay.n_z, lay.peers, lay.n_core
    n_tok, feats = tok.shape
    units = wg.shape[0]
    row_w = 2 * feats + LANES
    act_w = 3 * units + LANES
    term_w = feats + LANES
    half = 3 * units // 2
    act_half = ((act_w // LANES + 1) // 2) * LANES
    per = peers // 4
    far = n_z // 2
    y = lax.axis_index("dp")
    e = lax.axis_index("expert")
    x, z, core = e // (n_z * n_core), (e // n_core) % n_z, e % n_core
    me = x * n_core + core

    def place_of(peer, plane):
        return ((peer // n_core) * n_z + plane) * n_core + peer % n_core

    z_next = (y, place_of(me, (z + 1) % n_z))
    z_prev = (y, place_of(me, (z + n_z - 1) % n_z))
    y_next = ((y + 1) % 4, e)
    y_prev = ((y + 3) % 4, e)
    right_y, left_y, across_y = (y + 1) % 4, (y + 3) % 4, (y + 2) % 4

    def remote(src, dst, send_sem, recv_sem, device):
        return pltpu.make_async_remote_copy(
            src_ref=src, dst_ref=dst, send_sem=send_sem, recv_sem=recv_sem,
            device_id=device, device_id_type=MESH,
        )

    pending = []

    def go(copy):
        copy.start()
        pending.append(copy)
        return copy

    loads = [
        pltpu.make_async_copy(w, weights.at[pl.ds(i * units, units)], w_sem.at[i])
        for i, w in enumerate((wg, wu, wd))
    ]
    own = [
        pltpu.make_async_copy(tok, tok_all.at[0], own_sem.at[0]),
        pltpu.make_async_copy(cot, cot_all.at[0], own_sem.at[1]),
        pltpu.make_async_copy(aux, aux_all.at[0], own_sem.at[2]),
    ]
    for copy in own + loads:
        copy.start()

    barrier = pltpu.get_barrier_semaphore()
    for device in (y_next, y_prev):
        pl.semaphore_signal(barrier, inc=1, device_id=device, device_id_type=MESH)
    for k in range(1, n_z):
        pl.semaphore_signal(
            barrier, inc=1, device_id=(y, place_of(me, (z + k) % n_z)), device_id_type=MESH
        )
    for k in range(1, peers):
        pl.semaphore_signal(
            barrier, inc=1, device_id=(y, place_of((me + k) % peers, z)), device_id_type=MESH
        )
    pl.semaphore_wait(barrier, 2 + n_z - 1 + peers - 1)

    def z_span(hop, way):
        if hop < far:
            return pl.ds(0, n_tok)
        return pl.ds(0 if way == 0 else n_tok // 2, n_tok // 2)

    def z_hop(hop, way):
        sign = -1 if way == 0 else 1
        src_slot, dst_slot = (sign * (hop - 1)) % n_z, (sign * hop) % n_z
        span = z_span(hop, way)
        out = []
        for i, (mine, held) in enumerate(((tok, tok_all), (cot, cot_all))):
            src = mine.at[span] if hop == 1 else held.at[src_slot, span]
            out.append(
                remote(
                    src, held.at[dst_slot, span], ag_ss.at[way, hop - 1, i],
                    ag_rs.at[way, hop - 1, i], z_next if way == 0 else z_prev,
                )
            )
        return out

    arrived = {}

    def z_send(hop):
        for way in (0, 1):
            arrived[hop, way] = [go(copy) for copy in z_hop(hop, way)]

    def z_wait(hop, ways=(0, 1)):
        for way in ways:
            for copy in arrived[hop, way]:
                copy.wait_recv()

    aux_copies = {}

    def aux_send():
        for k in range(1, n_z):
            aux_copies[k] = go(
                remote(
                    aux, aux_all.at[k], aux_ss.at[k], aux_rs.at[k],
                    (y, place_of(me, (z + n_z - k) % n_z)),
                )
            )

    names = [place_of(j, z) for j in range(peers)]

    def read_table(slot):
        table = aux_all[slot]
        ids = table[0:8].astype(jnp.int32)
        return ids, table[8:16]

    def pick(pos, slot):
        ids, probs = read_table(slot)
        hits = jnp.concatenate(
            [jnp.sum(jnp.where(ids == n, 1.0, 0.0), axis=0, keepdims=True) for n in names], axis=0
        )
        given = [jnp.sum(jnp.where(ids == n, probs, 0.0), axis=0, keepdims=True) for n in names]
        before = (
            lax.broadcasted_iota(jnp.int32, (n_tok, n_tok), 0)
            < lax.broadcasted_iota(jnp.int32, (n_tok, n_tok), 1)
        )
        if peers % 8:
            hits_full = jnp.concatenate([hits, jnp.zeros((8 - peers, n_tok), F32)], axis=0)
        else:
            hits_full = hits
        rank = dot(hits_full.astype(BF16), jnp.where(before, 1.0, 0.0).astype(BF16), 1, 0)
        rank = jnp.where(hits > 0.5, rank[0:peers], -1.0)
        s_main = lax.broadcasted_iota(jnp.int32, (MAIN, n_tok), 0).astype(F32)
        s_spare = lax.broadcasted_iota(jnp.int32, (SPARE, n_tok), 0)
        main, main_p, spare, spare_p = [], [], [], []
        for j in range(peers):
            r = rank[j : j + 1]
            one = jnp.where(jnp.broadcast_to(r, (MAIN, n_tok)) == s_main, 1.0, 0.0)
            main.append(one)
            main_p.append(one * jnp.broadcast_to(given[j], (MAIN, n_tok)))
            over = jnp.where(r > MAIN - 0.5, 1.0, 0.0)
            sp = jnp.where(s_spare == slot, jnp.broadcast_to(over, (SPARE, n_tok)), 0.0)
            spare.append(sp)
            spare_p.append(sp * jnp.broadcast_to(given[j], (SPARE, n_tok)))
        one = jnp.concatenate(main, axis=0).astype(BF16)
        hot[pos] = one
        cols = pl.ds(slot * n_tok, n_tok)
        hot_spare[:, cols] = jnp.concatenate(spare, axis=0).astype(BF16)
        hot_spare_p[:, cols] = jnp.concatenate(spare_p, axis=0).astype(BF16)
        ones = jnp.ones((n_tok, LANES), BF16)
        shape = (peers, MAIN, -1)
        probs_rows = dot(jnp.concatenate(main_p, axis=0).astype(BF16), ones, 1, 0)
        sent[pos, :, :, 2 * feats :] = probs_rows.astype(BF16).reshape(peers, MAIN, LANES)
        sent[pos, :, :, 0:feats] = dot(one, tok_all[slot], 1, 0).astype(BF16).reshape(peers, MAIN, feats)
        sent[pos, :, :, feats : 2 * feats] = (
            dot(one, cot_all[slot], 1, 0).astype(BF16).reshape(peers, MAIN, feats)
        )

    def exchange(src, dst, send_sems, recv_sems, row):
        def copy_to(i):
            j = (me + i) % peers
            return remote(
                src.at[j], dst.at[me], send_sems.at[row, i], recv_sems.at[row, me],
                (y, place_of(j, z)),
            )

        def copy_from(i):
            j = (me + i) % peers
            return remote(
                src.at[j], dst.at[j], send_sems.at[row, i], recv_sems.at[row, j],
                (y, place_of(j, z)),
            )

        def start():
            @pl.loop(1, peers)
            def _(i):
                copy_to(i).start()

            dst[pl.ds(me, 1)] = src[pl.ds(me, 1)]

        def wait():
            @pl.loop(1, peers)
            def _(i):
                copy_from(i).wait_recv()

        def finish():
            @pl.loop(1, peers)
            def _(i):
                copy_to(i).wait_send()

        return types.SimpleNamespace(start=start, wait=wait, finish=finish)

    n_pos = len(lay.order)
    dispatch = {
        k: exchange(sent.at[p], rows.at[p], d_ss, d_rs, p) for k, p in lay.place.items()
    }
    dispatch_spare = exchange(sent_spare, rows_spare, d_ss, d_rs, n_pos)
    ret = {k: exchange(term.at[p], back.at[p], t_ss, t_rs, p) for k, p in lay.place.items()}
    ret_spare = exchange(term_spare, back_spare, t_ss, t_rs, n_pos)

    def gather(k):
        if k:
            aux_copies[k % n_z].wait_recv()
        pick(lay.place[k], k % n_z)
        dispatch[k].start()

    def gather_spare():
        ones = jnp.ones((n_z * n_tok, LANES), BF16)
        shape = (peers, SPARE)
        sent_spare[:, :, 2 * feats :] = (
            dot(hot_spare_p[...], ones, 1, 0).astype(BF16).reshape(shape + (LANES,))
        )
        for i, held in enumerate((tok_all, cot_all)):
            block = held[...].reshape(n_z * n_tok, feats)
            sent_spare[:, :, i * feats : (i + 1) * feats] = (
                dot(hot_spare[...], block, 1, 0).astype(BF16).reshape(shape + (feats,))
            )
        dispatch_spare.start()

    tile = min(256, units)

    def segment(r):
        ks, spare = lay.rounds[r]
        first_pos = lay.place[ks[0]]
        return pl.ds(first_pos, len(ks)), len(ks), spare

    y_copies = {}

    def y_send(kind, r, way, src, dst, src_spare, dst_spare, spare):
        device = y_next if way == 0 else y_prev
        made = [go(remote(src, dst, y_ss.at[kind, r, way], y_rs.at[kind, r, way], device))]
        if spare:
            made.append(
                go(remote(src_spare, dst_spare, yo_ss.at[kind, way], yo_rs.at[kind, way], device))
            )
        y_copies[kind, r, way] = made

    def y_wait(kind, r, way):
        for copy in y_copies[kind, r, way]:
            copy.wait_recv()

    def shard(index):
        return pl.ds(index * per, per)

    def project(r):
        span, n, spare = segment(r)
        for k in lay.rounds[r][0]:
            dispatch[k].wait()
        if spare:
            dispatch_spare.wait()
        if r == 0:
            for copy in loads:
                copy.wait()
        for base, count, col in ((0, 2 * units // tile, 0), (2 * units, units // tile, feats)):
            @pl.loop(0, count)
            def _(i):
                at = pl.multiple_of(base + i * tile, tile)
                block = weights[pl.ds(at, tile)]
                left = rows[span, :, :, col : col + feats].reshape(n * peers * MAIN, feats)
                out = dot(left, block, 1, 1).astype(BF16)
                part[span, :, :, pl.ds(at, tile)] = out.reshape(n, peers, MAIN, tile)
                if spare:
                    left = rows_spare[:, :, col : col + feats].reshape(peers * SPARE, feats)
                    out = dot(left, block, 1, 1).astype(BF16)
                    part_spare[:, :, pl.ds(at, tile)] = out.reshape(4, peers * SPARE // 4, tile)
        for way, cols in ((0, pl.ds(0, half)), (1, pl.ds(half, half))):
            y_send(
                0, r, way, part.at[span, shard(across_y), :, cols], first.at[way, span],
                part_spare.at[across_y, :, cols], first_spare.at[way], spare,
            )

    def fold(r):
        span, n, spare = segment(r)
        for way, cols, owner in ((0, pl.ds(0, half), right_y), (1, pl.ds(half, half), left_y)):
            y_wait(0, r, way)
            part[span, shard(owner), :, cols] = (
                part[span, shard(owner), :, cols].astype(F32) + first[way, span].astype(F32)
            ).astype(BF16)
            if spare:
                part_spare[pl.ds(owner, 1), :, cols] = (
                    part_spare[pl.ds(owner, 1), :, cols].astype(F32)
                    + first_spare[pl.ds(way, 1)].astype(F32)
                ).astype(BF16)
            y_send(
                1, r, way, part.at[span, shard(owner)], second.at[way, span],
                part_spare.at[owner], second_spare.at[way], spare,
            )

    def act_math(values, probs, units_w):
        gate, up, bck = values
        s = jax.nn.sigmoid(gate)
        silu = gate * s
        hidden = (silu * up).astype(BF16)
        pv = jnp.sum(hidden.astype(F32) * bck, axis=1, keepdims=True)
        p = jnp.concatenate([probs.astype(F32)] * (units_w // LANES), axis=1)
        gb = p * bck
        d_gate = (gb * up * s * (1.0 + gate * (1.0 - s))).astype(BF16)
        d_up = (gb * silu).astype(BF16)
        return hidden, d_gate, d_up, jnp.broadcast_to(pv, (pv.shape[0], LANES)).astype(BF16)

    def activate(r):
        span, n, spare = segment(r)
        y_wait(1, r, 0)
        y_wait(1, r, 1)
        count = n * per * MAIN

        def value(i):
            cols = pl.ds(i * units, units)
            return (
                part[span, shard(y), :, cols].astype(F32)
                + second[0, span, :, :, cols].astype(F32)
                + second[1, span, :, :, cols].astype(F32)
            ).reshape(count, units)

        probs = rows[span, shard(y), :, 2 * feats :].reshape(count, LANES)
        hidden, d_gate, d_up, pv = act_math([value(i) for i in range(3)], probs, units)
        for i, v in enumerate((hidden, d_gate, d_up)):
            acts[span, shard(y), :, i * units : (i + 1) * units] = v.reshape(n, per, MAIN, units)
        acts[span, shard(y), :, 3 * units :] = pv.reshape(n, per, MAIN, LANES)
        if spare:
            count = per * SPARE

            def value_spare(i):
                cols = pl.ds(i * units, units)
                return (
                    part_spare[pl.ds(y, 1), :, cols].astype(F32)
                    + second_spare[pl.ds(0, 1), :, cols].astype(F32)
                    + second_spare[pl.ds(1, 1), :, cols].astype(F32)
                ).reshape(count, units)

            probs = rows_spare[shard(y), :, 2 * feats :].reshape(count, LANES)
            hidden, d_gate, d_up, pv = act_math([value_spare(i) for i in range(3)], probs, units)
            for i, v in enumerate((hidden, d_gate, d_up)):
                acts_spare[pl.ds(y, 1), :, i * units : (i + 1) * units] = v.reshape(1, count, units)
            acts_spare[pl.ds(y, 1), :, 3 * units :] = pv.reshape(1, count, LANES)
        for way in (0, 1):
            y_send(
                2, r, way, acts.at[span, shard(y)], acts.at[span, shard(y)],
                acts_spare.at[y], acts_spare.at[y], spare,
            )

    def relay(r):
        span, n, spare = segment(r)
        for way, cols, owner in (
            (0, pl.ds(0, act_half), left_y), (1, pl.ds(act_half, act_w - act_half), right_y)
        ):
            y_wait(2, r, way)
            y_send(
                3, r, way, acts.at[span, shard(owner), :, cols], acts.at[span, shard(owner), :, cols],
                acts_spare.at[owner, :, cols], acts_spare.at[owner, :, cols], spare,
            )

    f_tile = min(256, feats)

    def send_back(r):
        span, n, spare = segment(r)
        y_wait(3, r, 0)
        y_wait(3, r, 1)

        @pl.loop(0, feats // f_tile)
        def _(i):
            at = pl.multiple_of(i * f_tile, f_tile)
            block = weights[0 : 2 * units, pl.ds(at, f_tile)]
            left = acts[span, :, :, units : 3 * units].reshape(n * peers * MAIN, 2 * units)
            term[span, :, :, pl.ds(at, f_tile)] = (
                dot(left, block, 1, 0).astype(BF16).reshape(n, peers, MAIN, f_tile)
            )
            if spare:
                left = acts_spare[:, :, units : 3 * units].reshape(peers * SPARE, 2 * units)
                term_spare[:, :, pl.ds(at, f_tile)] = (
                    dot(left, block, 1, 0).astype(BF16).reshape(peers, SPARE, f_tile)
                )

        term[span, :, :, feats:] = acts[span, :, :, 3 * units :]
        for k in lay.rounds[r][0]:
            ret[k].start()
        if spare:
            term_spare[:, :, feats:] = acts_spare[:, :, 3 * units :].reshape(peers, SPARE, LANES)
            ret_spare.start()

    z_copies = {}
    pg_copies = {}

    def wait_spare():
        ret_spare.wait()

    def combine(k):
        pos, slot = lay.place[k], k % n_z
        ret[k].wait()
        got = back[pos].reshape(peers * MAIN, term_w)
        got_spare = back_spare[...].reshape(peers * SPARE, term_w)
        one = hot[pos]
        spare = hot_spare[:, pl.ds(slot * n_tok, n_tok)]
        total = dot(one, got[:, 0:feats], 0, 0) + dot(spare, got_spare[:, 0:feats], 0, 0)
        ids, _ = read_table(slot)
        weighted = one.astype(F32) * got[:, feats:].astype(F32)
        weighted_spare = spare.astype(F32) * got_spare[:, feats:].astype(F32)
        grad = jnp.zeros((8, n_tok), F32)
        for j in range(peers):
            v = jnp.sum(weighted[j * MAIN : (j + 1) * MAIN], axis=0, keepdims=True)
            v = v + jnp.sum(weighted_spare[j * SPARE : (j + 1) * SPARE], axis=0, keepdims=True)
            grad = grad + jnp.where(ids == names[j], jnp.broadcast_to(v, (8, n_tok)), 0.0)
        if k == 0:
            pg_got[0] = grad
        else:
            pg_sent[slot] = grad
            pg_copies[slot] = go(
                remote(
                    pg_sent.at[slot], pg_got.at[n_z - slot], pg_ss.at[slot], pg_rs.at[n_z - slot],
                    (y, place_of(me, (z + slot) % n_z)),
                )
            )
        k_signed = k if k <= far else k - n_z
        if k_signed == far:
            z_sent[slot] = total.astype(BF16)
            lo, hi = pl.ds(0, n_tok // 2), pl.ds(n_tok // 2, n_tok // 2)
            z_copies[0, far] = go(
                remote(z_sent.at[slot, lo], z_right.at[far - 1, lo], z_ss.at[0, far],
                       z_rs.at[0, far - 1], z_next)
            )
            z_copies[1, far] = go(
                remote(z_sent.at[slot, hi], z_left.at[far - 1, hi], z_ss.at[1, far],
                       z_rs.at[1, far - 1], z_prev)
            )
            return
        h = n_tok // 2
        if k_signed != 0:
            way = 0 if k_signed > 0 else 1
            dist = abs(k_signed)
            z_copies[way, dist + 1].wait_recv()
            held = z_right if way == 0 else z_left
            if dist == far - 1:
                if way == 0:
                    z_sent[slot, 0:h] = (total[0:h] + held[dist, 0:h].astype(F32)).astype(BF16)
                    z_sent[slot, h:] = total[h:].astype(BF16)
                else:
                    z_sent[slot, h:] = (total[h:] + held[dist, h:].astype(F32)).astype(BF16)
                    z_sent[slot, 0:h] = total[0:h].astype(BF16)
            else:
                z_sent[slot] = (total + held[dist].astype(F32)).astype(BF16)
            z_copies[way, dist] = go(
                remote(z_sent.at[slot], held.at[dist - 1], z_ss.at[way, dist],
                       z_rs.at[way, dist - 1], z_next if way == 0 else z_prev)
            )
            return
        z_copies[0, 1].wait_recv()
        z_copies[1, 1].wait_recv()
        tg_out[...] = (total + z_right[0].astype(F32) + z_left[0].astype(F32)).astype(BF16)

    def finish_probs():
        for slot in pg_copies:
            pg_copies[slot].wait_recv()
        total = pg_got[0]
        for slot in range(1, n_z):
            total = total + pg_got[slot]
        pg_out[...] = total

    outs = [
        pltpu.make_async_copy(grads.at[pl.ds(i * units, units)], o, out_sem.at[i])
        for i, o in enumerate((gg_out, ug_out, dg_out))
    ]

    all_rows = n_pos * peers * MAIN

    def grads_in():
        left_full = rows[:, :, :, 0:feats].reshape(all_rows, feats)
        left_spare = rows_spare[:, :, 0:feats].reshape(peers * SPARE, feats)

        @pl.loop(0, 2 * units // tile)
        def _(i):
            at = pl.multiple_of(units + i * tile, tile)
            a = acts[:, :, :, pl.ds(at, tile)].reshape(all_rows, tile)
            b = acts_spare[:, :, pl.ds(at, tile)].reshape(peers * SPARE, tile)
            full = rows[:, :, :, 0:feats].reshape(all_rows, feats)
            spare = rows_spare[:, :, 0:feats].reshape(peers * SPARE, feats)
            grads[pl.ds(pl.multiple_of(i * tile, tile), tile)] = (
                dot(a, full, 0, 0) + dot(b, spare, 0, 0)
            ).astype(BF16)

        outs[0].start()
        outs[1].start()

    def scale():
        @pl.loop(0, n_pos)
        def _(i):
            p = rows[pl.ds(i, 1), :, :, 2 * feats :].astype(F32)
            p = jnp.concatenate([p] * (feats // LANES), axis=3)
            c = rows[pl.ds(i, 1), :, :, feats : 2 * feats].astype(F32)
            rows[pl.ds(i, 1), :, :, feats : 2 * feats] = (p * c).astype(BF16)

        p = jnp.concatenate([rows_spare[:, :, 2 * feats :].astype(F32)] * (feats // LANES), axis=2)
        c = rows_spare[:, :, feats : 2 * feats].astype(F32)
        rows_spare[:, :, feats : 2 * feats] = (p * c).astype(BF16)

    def grads_down():
        @pl.loop(0, units // tile)
        def _(i):
            at = pl.multiple_of(i * tile, tile)
            a = acts[:, :, :, pl.ds(at, tile)].reshape(all_rows, tile)
            b = acts_spare[:, :, pl.ds(at, tile)].reshape(peers * SPARE, tile)
            full = rows[:, :, :, feats : 2 * feats].reshape(all_rows, feats)
            spare = rows_spare[:, :, feats : 2 * feats].reshape(peers * SPARE, feats)
            grads[pl.ds(pl.multiple_of(2 * units + i * tile, tile), tile)] = (
                dot(a, full, 0, 0) + dot(b, spare, 0, 0)
            ).astype(BF16)

        outs[2].start()

    def own_wait():
        for copy in own:
            copy.wait()

    table = dict(
        aux_send=aux_send, z_send=z_send, z_wait=z_wait, own_wait=own_wait, gather=gather,
        gather_spare=gather_spare, project=project, fold=fold, activate=activate, relay=relay,
        send_back=send_back, wait_spare=wait_spare, combine=combine, finish_probs=finish_probs,
        grads_in=grads_in, scale=scale, grads_down=grads_down,
    )
    for name, *args in steps:
        table[name](*args)
    for copy in outs:
        copy.wait()
    for copy in pending:
        copy.wait_send()
    for group in (dispatch, ret):
        for item in group.values():
            item.finish()
    dispatch_spare.finish()
    ret_spare.finish()


def plan(n_z):
    if n_z == 4:
        rounds = [([0], False), ([2, 1], True), ([-1], False)]
        steps = [
            ("aux_send",), ("z_send", 1), ("own_wait",), ("gather", 0),
            ("z_wait", 1), ("z_send", 2), ("gather", 1), ("gather", -1), ("project", 0), ("fold", 0),
            ("activate", 0), ("z_wait", 2), ("gather", 2), ("gather_spare",), ("relay", 0),
            ("project", 1), ("fold", 1), ("send_back", 0), ("activate", 1), ("project", 2),
            ("relay", 1), ("fold", 2), ("send_back", 1), ("activate", 2), ("wait_spare",),
            ("combine", 2), ("combine", 1), ("relay", 2), ("scale",),
            ("send_back", 2), ("grads_in",), ("combine", -1), ("combine", 0), ("grads_down",),
            ("finish_probs",),
        ]
        return rounds, steps
    rounds = [
        ([0], False), ([1], False), ([2], False), ([3], False), ([4], True), ([-3], False), ([-2], False),
        ([-1], False),
    ]
    steps = [
        ("aux_send",), ("z_send", 1), ("own_wait",), ("gather", 0), ("project", 0), ("z_wait", 1),
        ("z_send", 2), ("fold", 0), ("gather", 1), ("activate", 0), ("gather", -1), ("project", 1),
        ("z_wait", 2), ("z_send", 3), ("gather", 2), ("fold", 1), ("gather", -2), ("activate", 1),
        ("project", 2), ("relay", 0), ("z_wait", 3), ("z_send", 4), ("gather", 3), ("fold", 2),
        ("project", 6), ("gather", -3), ("project", 7), ("activate", 2), ("project", 3), ("z_wait", 4),
        ("gather", 4), ("relay", 2), ("gather_spare",), ("fold", 3), ("project", 5), ("activate", 3),
        ("fold", 5), ("project", 4), ("relay", 3), ("scale",), ("fold", 4), ("activate", 5),
        ("activate", 4), ("send_back", 2), ("send_back", 0), ("relay", 5), ("send_back", 3), ("relay", 4),
        ("fold", 6), ("relay", 1), ("send_back", 4), ("activate", 6), ("send_back", 5), ("fold", 7),
        ("wait_spare",), ("combine", 4), ("send_back", 1), ("relay", 6), ("activate", 7), ("combine", 3),
        ("combine", -3), ("send_back", 6), ("relay", 7), ("combine", 2), ("combine", -2), ("send_back", 7),
        ("grads_in",), ("combine", 1), ("combine", -1), ("grads_down",), ("combine", 0), ("finish_probs",),
    ]
    return rounds, steps


def build(n_x, n_z, n_core):
    rounds, steps = plan(n_z)
    lay = make_layout(n_x, n_z, n_core, rounds)

    def local(tokens, cotangent, router_probs, expert_ids, w_gate, w_up, w_down):
        n_tok, feats = tokens.shape
        units = w_gate.shape[1]
        peers, n_pos, per = lay.peers, n_z, lay.peers // 4
        row_w, act_w, term_w = 2 * feats + LANES, 3 * units + LANES, feats + LANES
        extra = 8 - expert_ids.shape[1]
        aux = jnp.concatenate(
            [
                jnp.pad(expert_ids.T.astype(F32), ((0, extra), (0, 0)), constant_values=-1.0),
                jnp.pad(router_probs.T.astype(F32), ((0, extra), (0, 0))),
            ],
            axis=0,
        )
        half = 3 * units // 2
        spare_rows = peers * SPARE // 4
        dma = pltpu.SemaphoreType.DMA
        n_r = len(rounds)
        vm = pltpu.VMEM
        scratch = [
            vm((n_z, n_tok, feats), BF16), vm((n_z, n_tok, feats), BF16), vm((n_z, 16, n_tok), F32),
            vm((n_pos, peers * MAIN, n_tok), BF16), vm((peers * SPARE, n_z * n_tok), BF16),
            vm((peers * SPARE, n_z * n_tok), BF16),
            vm((n_pos, peers, MAIN, row_w), BF16), vm((peers, SPARE, row_w), BF16),
            vm((n_pos, peers, MAIN, row_w), BF16), vm((peers, SPARE, row_w), BF16),
            vm((3 * units, feats), BF16),
            vm((n_pos, peers, MAIN, 3 * units), BF16), vm((4, spare_rows, 3 * units), BF16),
            vm((2, n_pos, per, MAIN, half), BF16), vm((2, spare_rows, half), BF16),
            vm((2, n_pos, per, MAIN, 3 * units), BF16), vm((2, spare_rows, 3 * units), BF16),
            vm((n_pos, peers, MAIN, act_w), BF16), vm((4, spare_rows, act_w), BF16),
            vm((n_pos, peers, MAIN, term_w), BF16), vm((peers, SPARE, term_w), BF16),
            vm((n_pos, peers, MAIN, term_w), BF16), vm((peers, SPARE, term_w), BF16),
            vm((n_z, n_tok, feats), BF16), vm((n_z // 2, n_tok, feats), BF16),
            vm((n_z // 2, n_tok, feats), BF16),
            vm((n_z, 8, n_tok), F32), vm((n_z, 8, n_tok), F32), vm((3 * units, feats), BF16),
            dma((3,)), dma((3,)), dma((3,)), dma((n_z,)), dma((n_z,)),
            dma((2, n_z // 2, 2)), dma((2, n_z // 2, 2)),
            dma((n_pos + 1, peers)), dma((n_pos + 1, peers)),
            dma((4, n_r, 2)), dma((4, n_r, 2)), dma((4, 2)), dma((4, 2)),
            dma((n_pos + 1, peers)), dma((n_pos + 1, peers)),
            dma((2, n_z // 2 + 1)), dma((2, n_z // 2 + 1)), dma((n_z,)), dma((n_z,)),
        ]
        sds = jax.ShapeDtypeStruct
        anywhere = pl.BlockSpec(memory_space=pl.ANY)
        inside = pl.BlockSpec(memory_space=pltpu.VMEM)
        tg, pg, gg, ug, dg = pl.pallas_call(
            functools.partial(kernel, lay, steps),
            out_shape=(
                sds((n_tok, feats), BF16), sds((8, n_tok), F32), sds((units, feats), BF16),
                sds((units, feats), BF16), sds((units, feats), BF16),
            ),
            in_specs=[anywhere] * 6,
            out_specs=(inside, inside, anywhere, anywhere, anywhere),
            scratch_shapes=scratch,
            compiler_params=pltpu.CompilerParams(
                collective_id=0, has_side_effects=True, vmem_limit_bytes=63 * 1024 * 1024
            ),
        )(tokens, cotangent, aux, w_gate[0], w_up[0], w_down[0])
        return tg, pg[: expert_ids.shape[1]].T, gg[None], ug[None], dg[None]

    return local


def solution(mesh, shape=(4, 8, 2)):
    return jax.shard_map(
        build(*shape),
        mesh=mesh,
        in_specs=(
            P("expert", "dp"), P("expert", "dp"), P("expert", None), P("expert", None),
            P("expert", None, "dp"), P("expert", None, "dp"), P("expert", None, "dp"),
        ),
        out_specs=(
            P("expert", "dp"), P("expert", None),
            P("expert", None, "dp"), P("expert", None, "dp"), P("expert", None, "dp"),
        ),
        check_vma=False,
    )
```
